128 devices in a mesh: row: 8 (over x_hi, y), col: 16 (over z, x_lo, core).
Axes of the slice: x: 4 (x_hi: 2, x_lo: 2; x = x_hi * 2 + x_lo), y: 4, z: 4, core: 2. Of those that a mesh axis runs over, the one named last changes fastest.
Arguments:
- amplitudes: bfloat16 [32, 256, 32, 256], P('row', None, 'col'), may hold values from -6 to 6
- factors: bfloat16 [32, 256, 384], P('row'), may hold values from -0.109375 to 0.109375
- occ_energy: float32 [32], replicated, may hold values from -2 to -0.5
- vir_energy: float32 [256], replicated, may hold values from 0.2 to 3
Outputs:
- residual: float32 [32, 256, 32, 256], P('row', None, 'col')
The draws below stay inside these ranges and needn't reach their ends.
All inputs are finite; a program needn't handle non-finite values.
Results may differ from the reference program's by a relative error of at most 0.0029.
Values may be sent and summed in bfloat16 or wider, within the bound.
No kernel may reach another device: no remote copies, remote signals or barrier semaphores. Data moves between devices by JAX's collectives and lax.ppermute only.
A program may use at most 192 MiB of HBM per device.

```python
import math
import jax
import jax.numpy as jnp
from jax import lax

O = 32
V = 256
Q = 384


def block_scale(key, shape, shards, low, largest):
    def one(axis_at, parts):
        steps = jax.random.uniform(jax.random.fold_in(jax.random.fold_in(key, 6), axis_at), (parts,), jnp.float32, low / len(shards), largest / len(shards))
        return jnp.repeat(jnp.exp(steps), shape[axis_at] // parts).reshape((-1,) + (1,) * (len(shape) - axis_at - 1))

    factor_of = one(*shards[0])
    for cut in shards[1:]:
        factor_of = factor_of * one(*cut)
    return factor_of


def gaussian(own_key, shape, spread, limit, cuts=(), held_as=jnp.bfloat16):
    array = jax.random.normal(own_key, shape, jnp.float32) * spread
    if len(cuts) > 0:
        array = block_scale(own_key, shape, cuts, -0.22, 0.18) * array
    return jnp.clip(array, min=-limit, max=limit).astype(held_as)


def setup_inputs(seed: int = 0) -> dict:
    key_list = jax.random.split(jax.random.key(seed), 5)
    return {
        "amplitudes": gaussian(key_list[0], (O, V, O, V), 1.0, 6.0, ((0, 8), (2, 16))),
        "factors": gaussian(key_list[1], (O, V, Q), (8 * Q) ** -0.5, 0.109375, ((0, 8),)),
        "occ_energy": jnp.clip(jax.random.uniform(key_list[2], (O,), jnp.float32, -2.0, -0.5), -2.0, -0.5),
        "vir_energy": jnp.clip(jax.random.uniform(key_list[3], (V,), jnp.float32, 0.2, 3.0), 0.2, 3.0),
    }


def pair_term(left_factors, right_factors, amplitude_rows):
    left_count, virtual, auxiliary = left_factors.shape
    right_count = right_factors.shape[0]
    coulomb = jnp.dot(left_factors.reshape(left_count * virtual, auxiliary), right_factors.reshape(right_count * virtual, auxiliary).T, preferred_element_type=jnp.float32)
    exchange_part = jnp.einsum("icq,kaq->iakc", left_factors.astype(jnp.float32), right_factors.astype(jnp.float32), precision=lax.Precision.HIGHEST).reshape(left_count * virtual, right_count * virtual)
    coupling = (2.0 * coulomb - exchange_part).astype(jnp.bfloat16)
    return jnp.dot(coupling, amplitude_rows.reshape(right_count * virtual, -1), preferred_element_type=jnp.float32)


def reference(amplitudes, factors, occ_energy, vir_energy):
    group_size = math.gcd(O, 4)
    blocks = O // group_size
    factor_blocks = factors.reshape(blocks, group_size, V, Q)
    amplitude_blocks = amplitudes.reshape(blocks, group_size, V, O, V)

    def row_block(left_factors):
        def add_block(running, pieces):
            right_factors, amplitude_rows = pieces
            return running + pair_term(left_factors, right_factors, amplitude_rows), None

        start_value = jnp.zeros((group_size * V, O * V), jnp.float32)
        running, unused = lax.scan(add_block, start_value, (factor_blocks, amplitude_blocks))
        return running

    cycle_sum = lax.map(row_block, factor_blocks).reshape(O, V, O, V)
    mirrored = cycle_sum.transpose(2, 3, 0, 1)
    denominator = vir_energy[None, :, None, None] + vir_energy[None, None, None, :] - occ_energy[:, None, None, None] - occ_energy[None, None, :, None]
    return (cycle_sum + mirrored) / denominator
```

```python
import functools

import jax
import jax.numpy as jnp
from jax import lax
from jax.experimental import pallas as pl
from jax.experimental.pallas import tpu as pltpu
from jax.sharding import PartitionSpec as P

F32, BF16 = jnp.float32, jnp.bfloat16
VMEM = pl.BlockSpec(memory_space=pltpu.VMEM)
SMEM = pl.BlockSpec(memory_space=pltpu.SMEM)
AXES = ("row", "col")

X_HI, Y, Z, X_LO, CORE = 2, 4, 4, 2, 2


def permutation(move):
    pairs = []
    for x_hi in range(X_HI):
        for y in range(Y):
            for z in range(Z):
                for x_lo in range(X_LO):
                    for core in range(CORE):
                        h, w, d, l, c = move(x_hi, y, z, x_lo, core)
                        source = (x_hi * Y + y) * (Z * X_LO * CORE) + (z * X_LO + x_lo) * CORE + core
                        target = (h * Y + w) * (Z * X_LO * CORE) + (d * X_LO + l) * CORE + c
                        pairs.append((source, target))
    return pairs


def send(value, move):
    return lax.ppermute(value, AXES, permutation(move))


def along_y(step):
    return lambda h, y, z, l, c: (h, (y + step) % Y, z, l, c)


def other_half(h, y, z, l, c):
    return (1 - h, y, z, l, c)


def other_core(h, y, z, l, c):
    return (h, y, z, l, 1 - c)


def mirror(turn):
    def move(h, y, z, l, c):
        chip_row, chip_col = h * Y + y, z * X_LO + l
        return (chip_col // Y, chip_col % Y, chip_row // X_LO, chip_row % X_LO, (c + turn) % CORE)

    return move


def term_kernel(parts, has_sum, *refs):
    left, refs = refs[0], refs[1:]
    rights, refs = refs[:parts], refs[parts:]
    amps, refs = refs[:parts], refs[parts:]
    before = refs[0] if has_sum else None
    out, coupling = refs[-2], refs[-1]
    count, virtual, _ = left.shape

    def one(i, carry):
        own = left[i]
        rows = pl.ds(pl.multiple_of(i * virtual, virtual), virtual)
        total = before[rows, :] if has_sum else None
        at = 0
        for right, amp in zip(rights, amps):
            depth = right.shape[0]
            for k in range(depth):
                both = lax.dot_general(own, right[k], (((1,), (1,)), ((), ())), preferred_element_type=F32)
                coupling[:, (at + k) * virtual : (at + k + 1) * virtual] = (2.0 * both - both.T).astype(BF16)
            term = jnp.dot(
                coupling[:, at * virtual : (at + depth) * virtual], amp[...], preferred_element_type=F32
            )
            total = term if total is None else total + term
            at += depth
        out[rows, :] = total.astype(out.dtype)
        return carry

    lax.fori_loop(0, count, one, 0)


def terms(left, rights, amps, before=None, out_dtype=F32):
    count, virtual, aux = left.shape
    width = amps[0].shape[1]
    depth = sum(r.shape[0] for r in rights)
    operands = [left, *rights, *amps] + ([] if before is None else [before])
    return pl.pallas_call(
        functools.partial(term_kernel, len(rights), before is not None),
        out_shape=jax.ShapeDtypeStruct((count * virtual, width), out_dtype),
        in_specs=[VMEM] * len(operands),
        out_specs=VMEM,
        scratch_shapes=[pltpu.VMEM((virtual, depth * virtual), BF16)],
        input_output_aliases={} if before is None or out_dtype != F32 else {len(operands) - 1: 0},
        compiler_params=pltpu.CompilerParams(vmem_limit_bytes=12 << 20),
        cost_estimate=pl.CostEstimate(
            flops=2 * count * depth * virtual * virtual * (aux + width),
            bytes_accessed=2 * count * virtual * width * 4,
            transcendentals=0,
        ),
        name="terms",
    )(*operands)


def final_kernel(occ_first, occ_second, vir_col, vir_row, summed, received, first, second, out):
    rows, virtual = summed.shape[0], vir_col.shape[0]
    own_rows = rows // virtual
    for i in range(own_rows):
        side = (first, second)[i // 2]
        for j in range(2):
            block = (slice(i * virtual, (i + 1) * virtual), slice(j * virtual, (j + 1) * virtual))
            turned = side[j * virtual : (j + 1) * virtual, (i % 2) * virtual : (i % 2 + 1) * virtual]
            total = summed[block] + received[block].astype(F32) + turned.astype(F32).T
            denominator = vir_col[...] + vir_row[...] - occ_first[i] - occ_second[j]
            out[block] = total / denominator


def body(amplitudes, factors, occ_energy, vir_energy):
    own_rows, virtual, aux = factors.shape
    pairs_cols = amplitudes.shape[2]
    width = pairs_cols * virtual
    core = lax.axis_index("col") % CORE
    half = own_rows // 2

    mine = lax.dynamic_slice_in_dim(factors, core * half, half, 0)
    moved = [send(mine, other_half)] + [send(mine, along_y(s)) for s in (1, -1, 2)]
    swapped = send(jnp.stack(moved), other_core)
    whole = [
        jnp.where(core == 0, jnp.concatenate([m, s]), jnp.concatenate([s, m]))
        for m, s in zip(moved, swapped)
    ]
    left_other, right_prev, right_next, right_far = whole

    own = amplitudes.reshape(own_rows * virtual, width)
    cut = own_rows * virtual // 2
    prev = send(own, along_y(1))
    next_ = send(own, along_y(-1))
    far_top = send(prev[:cut], along_y(1))
    far_low = send(next_[cut:], along_y(-1))

    near = ([right_prev, right_next], [prev, next_])
    far = ([right_far[:half], right_far[half:]], [far_top, far_low])
    other = terms(left_other, [factors], [own])
    mine_sum = terms(factors, [factors], [own])
    other = terms(left_other, *near, other)
    mine_sum = terms(factors, *near, mine_sum)
    other = terms(left_other, *far, other, out_dtype=BF16)
    received = send(other, other_half)
    mine_sum = terms(factors, *far, mine_sum)

    rounded = (mine_sum + received.astype(F32)).astype(BF16)
    lower, upper = rounded[:cut], rounded[cut:]
    straight = send(jnp.where(core == 0, lower, upper), mirror(0))
    crossed = send(jnp.where(core == 0, upper, lower), mirror(1))
    first = jnp.where(core == 0, straight, crossed)
    second = jnp.where(core == 0, crossed, straight)

    occ_first = lax.dynamic_slice_in_dim(occ_energy, lax.axis_index("row") * own_rows, own_rows, 0)
    occ_second = lax.dynamic_slice_in_dim(occ_energy, lax.axis_index("col") * pairs_cols, pairs_cols, 0)
    out = pl.pallas_call(
        final_kernel,
        out_shape=jax.ShapeDtypeStruct((own_rows * virtual, width), F32),
        in_specs=[SMEM, SMEM] + [VMEM] * 6,
        out_specs=VMEM,
        compiler_params=pltpu.CompilerParams(vmem_limit_bytes=12 << 20),
        cost_estimate=pl.CostEstimate(flops=10 * own_rows * virtual * width, bytes_accessed=8 << 20, transcendentals=0),
        name="finish",
    )(occ_first, occ_second, vir_energy[:, None], vir_energy[None, :], mine_sum, received, first, second)
    return out.reshape(own_rows, virtual, pairs_cols, virtual)


def solution(mesh):
    in_specs = (P("row", None, "col", None), P("row", None, None), P(), P())
    out_specs = P("row", None, "col", None)
    return jax.shard_map(body, mesh=mesh, in_specs=in_specs, out_specs=out_specs, check_vma=False)
```

```python
import functools

import jax
import jax.numpy as jnp
from jax import lax
from jax.experimental import pallas as pl
from jax.experimental.pallas import tpu as pltpu
from jax.sharding import PartitionSpec as P


F32, BF16 = jnp.float32, jnp.bfloat16
VMEM = pl.BlockSpec(memory_space=pltpu.VMEM)
SMEM = pl.BlockSpec(memory_space=pltpu.SMEM)
AXES = ("row", "col")

X_HI, Y, Z, X_LO, CORE = 2, 4, 4, 2, 2


def permutation(move):
    pairs = []
    for x_hi in range(X_HI):
        for y in range(Y):
            for z in range(Z):
                for x_lo in range(X_LO):
                    for core in range(CORE):
                        h, w, d, l, c = move(x_hi, y, z, x_lo, core)
                        source = (x_hi * Y + y) * (Z * X_LO * CORE) + (z * X_LO + x_lo) * CORE + core
                        target = (h * Y + w) * (Z * X_LO * CORE) + (d * X_LO + l) * CORE + c
                        pairs.append((source, target))
    return pairs


def send(value, move):
    return lax.ppermute(value, AXES, permutation(move))


def along_y(step):
    return lambda h, y, z, l, c: (h, (y + step) % Y, z, l, c)


def other_half(h, y, z, l, c):
    return (1 - h, y, z, l, c)


def other_core(h, y, z, l, c):
    return (h, y, z, l, 1 - c)


def along_z(step):
    return lambda h, y, z, l, c: (h, y, (z + step) % Z, l, c)


def mirror_from(h, y, z, l, c):
    chip_row, chip_col = h * Y + y, z * X_LO + l
    return (chip_col // Y, chip_col % Y, chip_row // X_LO, chip_row % X_LO, c)


def turned_z(h, y, z, l):
    return z ^ ((l ^ (y % 2)) * 2 + h)


def spread(turn):
    return lambda h, y, z, l, c: (h, y, turned_z(h, y, z, l), l, c ^ turn)


def mirror_rest(h, y, z, l, c):
    return mirror_from(h, y, turned_z(h, y, z, l), l, c)


def mirror_whole(turn):
    return lambda h, y, z, l, c: mirror_from(h, y, z, l, c ^ turn)


def call(kernel, out_shape, operands, flops, specs=None, scratch=(), alias=None):
    return pl.pallas_call(
        kernel,
        out_shape=out_shape,
        in_specs=specs or [VMEM] * len(operands),
        out_specs=VMEM,
        scratch_shapes=scratch,
        input_output_aliases=alias or {},
        compiler_params=pltpu.CompilerParams(vmem_limit_bytes=6 << 20),
        cost_estimate=pl.CostEstimate(flops=flops, bytes_accessed=1 << 20, transcendentals=0),
    )(*operands)


def couple_all(left, right, out):
    left_count, virtual, aux = left.shape
    rows = left[...].reshape(left_count * virtual, aux)
    for k in range(right.shape[0]):
        both = lax.dot_general(rows, right[k], (((1,), (1,)), ((), ())), preferred_element_type=F32)
        for i in range(left_count):
            at = slice(i * virtual, (i + 1) * virtual)
            out[at, k * virtual : (k + 1) * virtual] = (2.0 * both[at] - both[at].T).astype(BF16)


def couple_whole_kernel(left, right, out):
    couple_all(left, right, out)


def fill_left(core, moved, swapped, left):
    half = moved.shape[0]
    left[pl.ds(core * half, half)] = moved[...]
    left[pl.ds((1 - core) * half, half)] = swapped[...]


def fill_right(core, z, moved, swapped, right):
    part = moved.shape[1]
    blocks = moved.shape[0] // Z
    for shift in range(Z):
        orbital = lax.rem(z - shift + Z, Z)
        for block in range(blocks):
            to = block * Z + orbital
            at = shift * blocks + block
            right[to, pl.ds(pl.multiple_of(core * part, part), part), :] = moved[at]
            right[to, pl.ds(pl.multiple_of((1 - core) * part, part), part), :] = swapped[at]


def couple_other_own_kernel(place, moved, swapped, right, out, left):
    fill_left(place[0], moved, swapped, left)
    couple_all(left, right, out)


def couple_other_rest_kernel(place, moved, swapped, right_moved, right_swapped, out, left, right):
    fill_left(place[0], moved, swapped, left)
    fill_right(place[0], place[1], right_moved, right_swapped, right)
    couple_all(left, right, out)


def couple_mine_rest_kernel(place, left, right_moved, right_swapped, out, right):
    fill_right(place[0], place[1], right_moved, right_swapped, right)
    couple_all(left, right, out)


def couple(kernel, operands, left_count, right_count, virtual, aux, scratch=()):
    shape = jax.ShapeDtypeStruct((left_count * virtual, right_count * virtual), BF16)
    flops = 2 * left_count * right_count * virtual * virtual * aux
    specs = [SMEM if o.dtype == jnp.int32 else VMEM for o in operands]
    scratch = [pltpu.VMEM((n, virtual, aux), BF16) for n in scratch]
    return call(kernel, shape, operands, flops, specs=specs, scratch=scratch)


def product_kernel(spans, has_sum, *refs):
    out = refs[-1]
    lefts, amps = refs[: len(spans)], refs[len(spans) : 2 * len(spans)]
    total = refs[-2][...] if has_sum else None
    for left, amp, (start, stop) in zip(lefts, amps, spans):
        term = jnp.dot(left[:, start:stop], amp[...], preferred_element_type=F32)
        total = term if total is None else total + term
    out[...] = total.astype(out.dtype)


def product(pieces, before=None, out_dtype=F32):
    lefts, starts, amps = zip(*pieces)
    spans = tuple((s, s + a.shape[0]) for s, a in zip(starts, amps))
    rows, width = lefts[0].shape[0], amps[0].shape[1]
    operands = [*lefts, *amps] + ([] if before is None else [before])
    alias = None if before is None or out_dtype != F32 else {len(operands) - 1: 0}
    flops = 2 * rows * width * sum(b - a for a, b in spans)
    kernel = functools.partial(product_kernel, spans, before is not None)
    return call(kernel, jax.ShapeDtypeStruct((rows, width), out_dtype), operands, flops, alias=alias)


def pack_kernel(*refs):
    parts, out = refs[:-1], refs[-1]
    size = parts[0].shape[0]
    for index, part in enumerate(parts):
        out[index * size : (index + 1) * size] = part[...]


def pack(parts):
    first = parts[0]
    shape = jax.ShapeDtypeStruct((len(parts) * first.shape[0], *first.shape[1:]), first.dtype)
    return call(pack_kernel, shape, parts, 1)


def spread_rows(value, out, index, lanes):
    virtual = value.shape[0]
    cuts = virtual // lanes
    for cut in range(cuts):
        out[pl.ds(cut * 2 + index, virtual, stride=2 * cuts), :] = value[:, cut * lanes : (cut + 1) * lanes]


def round_kernel(place, mine, received, same, other, turned):
    rows, virtual = mine.shape[0] // 2, mine.shape[1]
    for out, side in ((same, place[0]), (other, 1 - place[0])):
        for orbital in range(2):
            at = pl.ds(pl.multiple_of(side * rows + orbital * virtual, virtual), virtual)
            spread_rows((mine[at, :] + received[at, :].astype(F32)).T, turned, orbital, out.shape[1])
        out[...] = turned[...].astype(BF16)


def round_halves(place, mine, received, lanes):
    size = mine.size // 2
    half = jax.ShapeDtypeStruct((size // lanes, lanes), BF16)
    return pl.pallas_call(
        round_kernel,
        out_shape=[half, half],
        in_specs=[SMEM, VMEM, VMEM],
        out_specs=[VMEM, VMEM],
        scratch_shapes=[pltpu.VMEM(half.shape, F32)],
        compiler_params=pltpu.CompilerParams(vmem_limit_bytes=4 << 20),
        cost_estimate=pl.CostEstimate(flops=mine.size, bytes_accessed=6 * mine.size, transcendentals=0),
        name="round",
    )(place, mine, received)


def prepare_kernel(occ_first, occ_second, vir_col, vir_row, *refs):
    sums, received, base, inverse = refs[:2], refs[2:4], refs[4], refs[5]
    virtual = vir_col.shape[0]
    count = sums[0].shape[0] // virtual
    size = base.shape[0] // count
    for i in range(count):
        rows = slice(i * virtual, (i + 1) * virtual)
        for j in range(2):
            share = 1.0 / (vir_col[...] + vir_row[...] - occ_first[i] - occ_second[j])
            total = (sums[j][rows, :] + received[j][rows, :].astype(F32)) * share
            spread_rows(total, base.at[i * size : (i + 1) * size], j, base.shape[1])
            spread_rows(share, inverse.at[i * size : (i + 1) * size], j, base.shape[1])


def final_kernel(place, base, inverse, early_both, late_same, late_other, out):
    size = out.shape[0]
    early_same, early_other = early_both.at[:size], early_both.at[size:]
    step = pl.program_id(0)
    early = step < 2
    same = place[0] == lax.rem(step, 2)

    def finish(mirrored):
        out[...] = base[...] + mirrored[...].astype(F32) * inverse[...]

    for ref, first, own in (
        (early_same, True, True),
        (early_other, True, False),
        (late_same, False, True),
        (late_other, False, False),
    ):
        @pl.when((early == first) & (same == own))
        def _():
            finish(ref)


def inner(amplitudes, factors, occ_energy, vir_energy):
    own_rows, virtual, aux = factors.shape
    pairs_cols = amplitudes.shape[2]
    row, col = lax.axis_index("row"), lax.axis_index("col")
    core, z = lax.rem(col, CORE), col // (X_LO * CORE)
    place = jnp.stack([core, z])
    depth = own_rows * virtual
    half, part = own_rows // 2, virtual // CORE

    piece = lax.dynamic_slice(factors, (z, core * part, 0), (1, part, aux))
    pieces = [send(piece, along_y(s)) for s in (1, -1, 2)]
    left_moved = send(lax.dynamic_slice_in_dim(factors, core * half, half, 0), other_half)

    whole = amplitudes.reshape(depth, pairs_cols * virtual)
    own = [whole[:, j * virtual : (j + 1) * virtual] for j in range(pairs_cols)]
    prev, next_ = [], []
    for j in range(pairs_cols):
        prev.append(send(own[j], along_y(1)))
        next_.append(send(own[j], along_y(-1)))
    pieces = pack(pieces)
    eighths = [pieces] + [send(pieces, along_z(s)) for s in (1, 2, 3)]
    left_swapped = send(left_moved, other_core)
    right_moved = pack(eighths)
    right_swapped = send(right_moved, other_core)
    far = [send(prev[0], along_y(1))]
    far.append(send(next_[1], along_y(-1)))

    count, rest = own_rows, 3 * own_rows
    coupling = {}
    coupling["mine", "own"] = couple(couple_whole_kernel, [factors, factors], count, count, virtual, aux)
    coupling["other", "own"] = couple(
        couple_other_own_kernel, [place, left_moved, left_swapped, factors], count, count, virtual, aux, (count,)
    )
    operands = [place, left_moved, left_swapped, right_moved, right_swapped]
    coupling["other", "rest"] = couple(
        couple_other_rest_kernel, operands, count, rest, virtual, aux, (count, rest)
    )
    operands = [place, factors, right_moved, right_swapped]
    coupling["mine", "rest"] = couple(couple_mine_rest_kernel, operands, count, rest, virtual, aux, (rest,))

    def sums_of(name, j, dtype):
        rest = coupling[name, "rest"]
        pieces = [(rest, 0, prev[j]), (rest, depth, next_[j]), (rest, 2 * depth, far[j])]
        return product([(coupling[name, "own"], 0, own[j]), *pieces], None, dtype)

    sums, received, mirrored = [], [], []
    for j in range(pairs_cols):
        other = sums_of("other", j, BF16)
        received.append(send(other, other_half))
        sums.append(sums_of("mine", j, F32))
    lanes = 128
    cuts = virtual // lanes
    for j in range(pairs_cols):
        same, other = round_halves(place, sums[j], received[j], lanes)
        if j == 0:
            halves = [send(same, spread(0)), send(other, spread(1))]
            mirrored.append(send(pack(halves), mirror_rest))
            continue
        mirrored += [send(same, mirror_whole(0)), send(other, mirror_whole(1))]

    occ_first = lax.dynamic_slice_in_dim(occ_energy, row * own_rows, own_rows, 0)
    occ_second = lax.dynamic_slice_in_dim(occ_energy, col * pairs_cols, pairs_cols, 0)
    shape = jax.ShapeDtypeStruct((depth * cuts * pairs_cols, lanes), F32)
    operands = [vir_energy[:, None], vir_energy[None, :], *sums, *received]
    base, inverse = pl.pallas_call(
        prepare_kernel,
        out_shape=[shape, shape],
        in_specs=[SMEM] * 2 + [VMEM] * len(operands),
        out_specs=[VMEM, VMEM],
        compiler_params=pltpu.CompilerParams(vmem_limit_bytes=4 << 20),
        cost_estimate=pl.CostEstimate(flops=4 * shape.size, bytes_accessed=10 * shape.size, transcendentals=0),
        name="prepare",
    )(occ_first, occ_second, *operands)
    block = shape.shape[0] // own_rows

    def orbital_of(step, place):
        return (lax.rem(step, 2) * 2 + step // 2, 0)

    by_orbital = pl.BlockSpec((block, lanes), orbital_of)
    out = pl.pallas_call(
        final_kernel,
        out_shape=shape,
        grid_spec=pltpu.PrefetchScalarGridSpec(
            num_scalar_prefetch=1,
            grid=(own_rows,),
            in_specs=[by_orbital] * 2 + [pl.BlockSpec(m.shape, lambda step, place: (0, 0)) for m in mirrored],
            out_specs=by_orbital,
        ),
        compiler_params=pltpu.CompilerParams(vmem_limit_bytes=12 << 20),
        cost_estimate=pl.CostEstimate(flops=2 * shape.size, bytes_accessed=12 * shape.size, transcendentals=0),
        name="finish",
    )(place, base, inverse, *mirrored)
    out = out.reshape(own_rows, virtual, cuts, pairs_cols, lanes).transpose(0, 1, 3, 2, 4)
    return out.reshape(own_rows, virtual, pairs_cols, virtual)


def solution(mesh):
    in_specs = (P("row", None, "col", None), P("row", None, None), P(), P())
    out_specs = P("row", None, "col", None)
    return jax.shard_map(inner, mesh=mesh, in_specs=in_specs, out_specs=out_specs, check_vma=False)
```

```python
import functools

import jax
import jax.numpy as jnp
from jax import lax
from jax.experimental import pallas as pl
from jax.experimental.pallas import tpu as pltpu
from jax.sharding import PartitionSpec as P


F32, BF16 = jnp.float32, jnp.bfloat16
VMEM = pl.BlockSpec(memory_space=pltpu.VMEM)
SMEM = pl.BlockSpec(memory_space=pltpu.SMEM)
AXES = ("row", "col")

X_HI, Y, Z, X_LO, CORE = 2, 4, 4, 2, 2


def permutation(move):
    pairs = []
    for x_hi in range(X_HI):
        for y in range(Y):
            for z in range(Z):
                for x_lo in range(X_LO):
                    for core in range(CORE):
                        h, w, d, l, c = move(x_hi, y, z, x_lo, core)
                        source = (x_hi * Y + y) * (Z * X_LO * CORE) + (z * X_LO + x_lo) * CORE + core
                        target = (h * Y + w) * (Z * X_LO * CORE) + (d * X_LO + l) * CORE + c
                        pairs.append((source, target))
    return pairs


def send(value, move):
    return lax.ppermute(value, AXES, permutation(move))


def along_y(step):
    return lambda h, y, z, l, c: (h, (y + step) % Y, z, l, c)


def other_half(h, y, z, l, c):
    return (1 - h, y, z, l, c)


def other_core(h, y, z, l, c):
    return (h, y, z, l, 1 - c)


def along_z(step):
    return lambda h, y, z, l, c: (h, y, (z + step) % Z, l, c)


def mirror_from(h, y, z, l, c):
    chip_row, chip_col = h * Y + y, z * X_LO + l
    return (chip_col // Y, chip_col % Y, chip_row // X_LO, chip_row % X_LO, c)


def turned_z(h, y, z, l):
    return z ^ ((l ^ (y % 2)) * 2 + h)


def spread(turn):
    return lambda h, y, z, l, c: (h, y, turned_z(h, y, z, l), l, c ^ turn)


def mirror_rest(h, y, z, l, c):
    return mirror_from(h, y, turned_z(h, y, z, l), l, c)


def mirror_whole(turn):
    return lambda h, y, z, l, c: mirror_from(h, y, z, l, c ^ turn)


def call(kernel, out_shape, operands, flops, specs=None, scratch=(), alias=None):
    return pl.pallas_call(
        kernel,
        out_shape=out_shape,
        in_specs=specs or [VMEM] * len(operands),
        out_specs=VMEM,
        scratch_shapes=scratch,
        input_output_aliases=alias or {},
        compiler_params=pltpu.CompilerParams(vmem_limit_bytes=6 << 20),
        cost_estimate=pl.CostEstimate(flops=flops, bytes_accessed=1 << 20, transcendentals=0),
    )(*operands)


def couple_all(left, right, out):
    left_count, virtual, aux = left.shape
    rows = left[...].reshape(left_count * virtual, aux)
    for k in range(right.shape[0]):
        both = lax.dot_general(rows, right[k], (((1,), (1,)), ((), ())), preferred_element_type=F32)
        for i in range(left_count):
            at = slice(i * virtual, (i + 1) * virtual)
            out[at, k * virtual : (k + 1) * virtual] = (2.0 * both[at] - both[at].T).astype(BF16)


def couple_whole_kernel(left, right, out):
    couple_all(left, right, out)


def fill_left(core, moved, swapped, left):
    half = moved.shape[0]
    left[pl.ds(core * half, half)] = moved[...]
    left[pl.ds((1 - core) * half, half)] = swapped[...]


def fill_right(core, z, moved, swapped, right):
    part = moved.shape[1]
    blocks = moved.shape[0] // Z
    for shift in range(Z):
        orbital = lax.rem(z - shift + Z, Z)
        for block in range(blocks):
            to = block * Z + orbital
            at = shift * blocks + block
            right[to, pl.ds(pl.multiple_of(core * part, part), part), :] = moved[at]
            right[to, pl.ds(pl.multiple_of((1 - core) * part, part), part), :] = swapped[at]


def couple_other_own_kernel(place, moved, swapped, right, out, left):
    fill_left(place[0], moved, swapped, left)
    couple_all(left, right, out)


def couple_other_rest_kernel(place, moved, swapped, right_moved, right_swapped, out, left, right):
    fill_left(place[0], moved, swapped, left)
    fill_right(place[0], place[1], right_moved, right_swapped, right)
    couple_all(left, right, out)


def couple_mine_rest_kernel(place, left, right_moved, right_swapped, out, right):
    fill_right(place[0], place[1], right_moved, right_swapped, right)
    couple_all(left, right, out)


def couple(kernel, operands, left_count, right_count, virtual, aux, scratch=()):
    shape = jax.ShapeDtypeStruct((left_count * virtual, right_count * virtual), BF16)
    flops = 2 * left_count * right_count * virtual * virtual * aux
    specs = [SMEM if o.dtype == jnp.int32 else VMEM for o in operands]
    scratch = [pltpu.VMEM((n, virtual, aux), BF16) for n in scratch]
    return call(kernel, shape, operands, flops, specs=specs, scratch=scratch)


def product_kernel(spans, has_sum, *refs):
    out = refs[-1]
    lefts, amps = refs[: len(spans)], refs[len(spans) : 2 * len(spans)]
    total = refs[-2][...] if has_sum else None
    for left, amp, (start, stop) in zip(lefts, amps, spans):
        term = jnp.dot(left[:, start:stop], amp[...], preferred_element_type=F32)
        total = term if total is None else total + term
    out[...] = total.astype(out.dtype)


def product(pieces, before=None, out_dtype=F32):
    lefts, starts, amps = zip(*pieces)
    spans = tuple((s, s + a.shape[0]) for s, a in zip(starts, amps))
    rows, width = lefts[0].shape[0], amps[0].shape[1]
    operands = [*lefts, *amps] + ([] if before is None else [before])
    alias = None if before is None or out_dtype != F32 else {len(operands) - 1: 0}
    flops = 2 * rows * width * sum(b - a for a, b in spans)
    kernel = functools.partial(product_kernel, spans, before is not None)
    return call(kernel, jax.ShapeDtypeStruct((rows, width), out_dtype), operands, flops, alias=alias)


def pack_kernel(*refs):
    parts, out = refs[:-1], refs[-1]
    size = parts[0].shape[0]
    for index, part in enumerate(parts):
        out[index * size : (index + 1) * size] = part[...]


def pack(parts):
    first = parts[0]
    shape = jax.ShapeDtypeStruct((len(parts) * first.shape[0], *first.shape[1:]), first.dtype)
    return call(pack_kernel, shape, parts, 1)


def spread_rows(value, out, index, lanes):
    virtual = value.shape[0]
    cuts = virtual // lanes
    for cut in range(cuts):
        out[pl.ds(cut * 2 + index, virtual, stride=2 * cuts), :] = value[:, cut * lanes : (cut + 1) * lanes]


def round_kernel(place, mine, received, same, other, turned):
    rows, virtual = mine.shape[0] // 2, mine.shape[1]
    for out, side in ((same, place[0]), (other, 1 - place[0])):
        for orbital in range(2):
            at = pl.ds(pl.multiple_of(side * rows + orbital * virtual, virtual), virtual)
            spread_rows((mine[at, :] + received[at, :].astype(F32)).T, turned, orbital, out.shape[1])
        out[...] = turned[...].astype(BF16)


def round_halves(place, mine, received, lanes):
    size = mine.size // 2
    half = jax.ShapeDtypeStruct((size // lanes, lanes), BF16)
    return pl.pallas_call(
        round_kernel,
        out_shape=[half, half],
        in_specs=[SMEM, VMEM, VMEM],
        out_specs=[VMEM, VMEM],
        scratch_shapes=[pltpu.VMEM(half.shape, F32)],
        compiler_params=pltpu.CompilerParams(vmem_limit_bytes=4 << 20),
        cost_estimate=pl.CostEstimate(flops=mine.size, bytes_accessed=6 * mine.size, transcendentals=0),
        name="round",
    )(place, mine, received)


def prepare_kernel(occ_first, occ_second, vir_col, vir_row, *refs):
    sums, received, base, inverse = refs[:2], refs[2:4], refs[4], refs[5]
    virtual = vir_col.shape[0]
    count = sums[0].shape[0] // virtual
    size = base.shape[0] // count
    for i in range(count):
        rows = slice(i * virtual, (i + 1) * virtual)
        for j in range(2):
            share = 1.0 / (vir_col[...] + vir_row[...] - occ_first[i] - occ_second[j])
            total = (sums[j][rows, :] + received[j][rows, :].astype(F32)) * share
            spread_rows(total, base.at[i * size : (i + 1) * size], j, base.shape[1])
            spread_rows(share, inverse.at[i * size : (i + 1) * size], j, base.shape[1])


def final_kernel(place, base, inverse, early_both, late_same, late_other, out):
    size = late_same.shape[0]
    for orbital in range(out.shape[0] // size):
        rows = slice(orbital * size, (orbital + 1) * size)
        same = place[0] == orbital // 2
        if orbital % 2 == 0:
            first = pl.ds(pl.multiple_of(jnp.where(same, 0, size), size), size)
            out[rows, :] = base[rows, :] + early_both[first, :].astype(F32) * inverse[rows, :]
            continue

        @pl.when(same)
        def _():
            out[rows, :] = base[rows, :] + late_same[...].astype(F32) * inverse[rows, :]

        @pl.when(jnp.logical_not(same))
        def _():
            out[rows, :] = base[rows, :] + late_other[...].astype(F32) * inverse[rows, :]


def inner(amplitudes, factors, occ_energy, vir_energy):
    own_rows, virtual, aux = factors.shape
    pairs_cols = amplitudes.shape[2]
    row, col = lax.axis_index("row"), lax.axis_index("col")
    core, z = lax.rem(col, CORE), col // (X_LO * CORE)
    place = jnp.stack([core, z])
    depth = own_rows * virtual
    half, part = own_rows // 2, virtual // CORE

    piece = lax.dynamic_slice(factors, (z, core * part, 0), (1, part, aux))
    pieces = [send(piece, along_y(s)) for s in (1, -1, 2)]
    left_moved = send(lax.dynamic_slice_in_dim(factors, core * half, half, 0), other_half)

    whole = amplitudes.reshape(depth, pairs_cols * virtual)
    own = [whole[:, j * virtual : (j + 1) * virtual] for j in range(pairs_cols)]
    prev, next_ = [], []
    for j in range(pairs_cols):
        prev.append(send(own[j], along_y(1)))
        next_.append(send(own[j], along_y(-1)))
    pieces = pack(pieces)
    eighths = [pieces] + [send(pieces, along_z(s)) for s in (1, 2, 3)]
    left_swapped = send(left_moved, other_core)
    right_moved = pack(eighths)
    right_swapped = send(right_moved, other_core)
    far = [send(prev[0], along_y(1))]
    far.append(send(next_[1], along_y(-1)))

    count, rest = own_rows, 3 * own_rows
    coupling = {}
    coupling["mine", "own"] = couple(couple_whole_kernel, [factors, factors], count, count, virtual, aux)
    coupling["other", "own"] = couple(
        couple_other_own_kernel, [place, left_moved, left_swapped, factors], count, count, virtual, aux, (count,)
    )
    operands = [place, left_moved, left_swapped, right_moved, right_swapped]
    coupling["other", "rest"] = couple(
        couple_other_rest_kernel, operands, count, rest, virtual, aux, (count, rest)
    )
    operands = [place, factors, right_moved, right_swapped]
    coupling["mine", "rest"] = couple(couple_mine_rest_kernel, operands, count, rest, virtual, aux, (rest,))

    def sums_of(name, j, dtype):
        rest = coupling[name, "rest"]
        pieces = [(rest, 0, prev[j]), (rest, depth, next_[j]), (rest, 2 * depth, far[j])]
        return product([(coupling[name, "own"], 0, own[j]), *pieces], None, dtype)

    sums, received, mirrored = [], [], []
    for j in range(pairs_cols):
        other = sums_of("other", j, BF16)
        received.append(send(other, other_half))
        sums.append(sums_of("mine", j, F32))
    lanes = 128
    cuts = virtual // lanes
    for j in range(pairs_cols):
        same, other = round_halves(place, sums[j], received[j], lanes)
        if j == 0:
            halves = [send(same, spread(0)), send(other, spread(1))]
            mirrored.append(send(pack(halves), mirror_rest))
            continue
        mirrored += [send(same, mirror_whole(0)), send(other, mirror_whole(1))]

    occ_first = lax.dynamic_slice_in_dim(occ_energy, row * own_rows, own_rows, 0)
    occ_second = lax.dynamic_slice_in_dim(occ_energy, col * pairs_cols, pairs_cols, 0)
    shape = jax.ShapeDtypeStruct((depth * cuts * pairs_cols, lanes), F32)
    operands = [vir_energy[:, None], vir_energy[None, :], *sums, *received]
    base, inverse = pl.pallas_call(
        prepare_kernel,
        out_shape=[shape, shape],
        in_specs=[SMEM] * 2 + [VMEM] * len(operands),
        out_specs=[VMEM, VMEM],
        compiler_params=pltpu.CompilerParams(vmem_limit_bytes=4 << 20),
        cost_estimate=pl.CostEstimate(flops=4 * shape.size, bytes_accessed=10 * shape.size, transcendentals=0),
        name="prepare",
    )(occ_first, occ_second, *operands)
    operands = [place, base, inverse, *mirrored]
    specs = [SMEM] + [VMEM] * (len(operands) - 1)
    out = call(final_kernel, shape, operands, 2 * shape.size, specs=specs)
    out = out.reshape(own_rows, virtual, cuts, pairs_cols, lanes).transpose(0, 1, 3, 2, 4)
    return out.reshape(own_rows, virtual, pairs_cols, virtual)


def solution(mesh):
    in_specs = (P("row", None, "col", None), P("row", None, None), P(), P())
    out_specs = P("row", None, "col", None)
    return jax.shard_map(inner, mesh=mesh, in_specs=in_specs, out_specs=out_specs, check_vma=False)
```

```python
import functools

import jax
import jax.numpy as jnp
from jax import lax
from jax.experimental import pallas as pl
from jax.experimental.pallas import tpu as pltpu
from jax.sharding import PartitionSpec as P


F32, BF16 = jnp.float32, jnp.bfloat16
VMEM = pl.BlockSpec(memory_space=pltpu.VMEM)
SMEM = pl.BlockSpec(memory_space=pltpu.SMEM)
AXES = ("row", "col")

X_HI, Y, Z, X_LO, CORE = 2, 4, 4, 2, 2


def permutation(move):
    pairs = []
    for x_hi in range(X_HI):
        for y in range(Y):
            for z in range(Z):
                for x_lo in range(X_LO):
                    for core in range(CORE):
                        h, w, d, l, c = move(x_hi, y, z, x_lo, core)
                        source = (x_hi * Y + y) * (Z * X_LO * CORE) + (z * X_LO + x_lo) * CORE + core
                        target = (h * Y + w) * (Z * X_LO * CORE) + (d * X_LO + l) * CORE + c
                        pairs.append((source, target))
    return pairs


def send(value, move):
    return lax.ppermute(value, AXES, permutation(move))


def along_y(step):
    return lambda h, y, z, l, c: (h, (y + step) % Y, z, l, c)


def other_half(h, y, z, l, c):
    return (1 - h, y, z, l, c)


def other_core(h, y, z, l, c):
    return (h, y, z, l, 1 - c)


def along_z(step):
    return lambda h, y, z, l, c: (h, y, (z + step) % Z, l, c)


def mirror_from(h, y, z, l, c):
    chip_row, chip_col = h * Y + y, z * X_LO + l
    return (chip_col // Y, chip_col % Y, chip_row // X_LO, chip_row % X_LO, c)


def turned_z(h, y, z, l):
    return z ^ ((l ^ (y % 2)) * 2 + h)


def spread(turn):
    return lambda h, y, z, l, c: (h, y, turned_z(h, y, z, l), l, c ^ turn)


def mirror_rest(h, y, z, l, c):
    return mirror_from(h, y, turned_z(h, y, z, l), l, c)


def mirror_whole(turn):
    return lambda h, y, z, l, c: mirror_from(h, y, z, l, c ^ turn)


def call(kernel, out_shape, operands, flops, specs=None, scratch=(), alias=None):
    return pl.pallas_call(
        kernel,
        out_shape=out_shape,
        in_specs=specs or [VMEM] * len(operands),
        out_specs=VMEM,
        scratch_shapes=scratch,
        input_output_aliases=alias or {},
        compiler_params=pltpu.CompilerParams(vmem_limit_bytes=6 << 20),
        cost_estimate=pl.CostEstimate(flops=flops, bytes_accessed=1 << 20, transcendentals=0),
    )(*operands)


def couple_all(left, right, out):
    left_count, virtual, aux = left.shape
    rows = left[...].reshape(left_count * virtual, aux)
    for k in range(right.shape[0]):
        both = lax.dot_general(rows, right[k], (((1,), (1,)), ((), ())), preferred_element_type=F32)
        for i in range(left_count):
            at = slice(i * virtual, (i + 1) * virtual)
            out[at, k * virtual : (k + 1) * virtual] = (2.0 * both[at] - both[at].T).astype(BF16)


def couple_whole_kernel(left, right, out):
    couple_all(left, right, out)


def fill_left(core, moved, swapped, left):
    half = moved.shape[0]
    left[pl.ds(core * half, half)] = moved[...]
    left[pl.ds((1 - core) * half, half)] = swapped[...]


def fill_right(core, z, moved, swapped, right):
    part = moved.shape[1]
    blocks = moved.shape[0] // Z
    for shift in range(Z):
        orbital = lax.rem(z - shift + Z, Z)
        for block in range(blocks):
            to = block * Z + orbital
            at = shift * blocks + block
            right[to, pl.ds(pl.multiple_of(core * part, part), part), :] = moved[at]
            right[to, pl.ds(pl.multiple_of((1 - core) * part, part), part), :] = swapped[at]


def couple_other_own_kernel(place, moved, swapped, right, out, left):
    fill_left(place[0], moved, swapped, left)
    couple_all(left, right, out)


def couple_other_rest_kernel(place, moved, swapped, right_moved, right_swapped, out, left, right):
    fill_left(place[0], moved, swapped, left)
    fill_right(place[0], place[1], right_moved, right_swapped, right)
    couple_all(left, right, out)


def couple_mine_rest_kernel(place, left, right_moved, right_swapped, out, right):
    fill_right(place[0], place[1], right_moved, right_swapped, right)
    couple_all(left, right, out)


def couple(kernel, operands, left_count, right_count, virtual, aux, scratch=()):
    shape = jax.ShapeDtypeStruct((left_count * virtual, right_count * virtual), BF16)
    flops = 2 * left_count * right_count * virtual * virtual * aux
    specs = [SMEM if o.dtype == jnp.int32 else VMEM for o in operands]
    scratch = [pltpu.VMEM((n, virtual, aux), BF16) for n in scratch]
    return call(kernel, shape, operands, flops, specs=specs, scratch=scratch)


def product_kernel(spans, has_sum, *refs):
    out = refs[-1]
    lefts, amps = refs[: len(spans)], refs[len(spans) : 2 * len(spans)]
    total = refs[-2][...] if has_sum else None
    for left, amp, (start, stop) in zip(lefts, amps, spans):
        term = jnp.dot(left[:, start:stop], amp[...], preferred_element_type=F32)
        total = term if total is None else total + term
    out[...] = total.astype(out.dtype)


def product(pieces, before=None, out_dtype=F32):
    lefts, starts, amps = zip(*pieces)
    spans = tuple((s, s + a.shape[0]) for s, a in zip(starts, amps))
    rows, width = lefts[0].shape[0], amps[0].shape[1]
    operands = [*lefts, *amps] + ([] if before is None else [before])
    alias = None if before is None or out_dtype != F32 else {len(operands) - 1: 0}
    flops = 2 * rows * width * sum(b - a for a, b in spans)
    kernel = functools.partial(product_kernel, spans, before is not None)
    return call(kernel, jax.ShapeDtypeStruct((rows, width), out_dtype), operands, flops, alias=alias)


def pack_kernel(*refs):
    parts, out = refs[:-1], refs[-1]
    size = parts[0].shape[0]
    for index, part in enumerate(parts):
        out[index * size : (index + 1) * size] = part[...]


def pack(parts):
    first = parts[0]
    shape = jax.ShapeDtypeStruct((len(parts) * first.shape[0], *first.shape[1:]), first.dtype)
    return call(pack_kernel, shape, parts, 1)


def spread_rows(value, out, index, lanes):
    virtual = value.shape[0]
    cuts = virtual // lanes
    for cut in range(cuts):
        out[pl.ds(cut * 2 + index, virtual, stride=2 * cuts), :] = value[:, cut * lanes : (cut + 1) * lanes]


def round_kernel(place, mine, received, same, other, turned):
    rows, virtual = mine.shape[0] // 2, mine.shape[1]
    for out, side in ((same, place[0]), (other, 1 - place[0])):
        for orbital in range(2):
            at = pl.ds(pl.multiple_of(side * rows + orbital * virtual, virtual), virtual)
            spread_rows((mine[at, :] + received[at, :].astype(F32)).T, turned, orbital, out.shape[1])
        out[...] = turned[...].astype(BF16)


def round_halves(place, mine, received, lanes):
    size = mine.size // 2
    half = jax.ShapeDtypeStruct((size // lanes, lanes), BF16)
    return pl.pallas_call(
        round_kernel,
        out_shape=[half, half],
        in_specs=[SMEM, VMEM, VMEM],
        out_specs=[VMEM, VMEM],
        scratch_shapes=[pltpu.VMEM(half.shape, F32)],
        compiler_params=pltpu.CompilerParams(vmem_limit_bytes=4 << 20),
        cost_estimate=pl.CostEstimate(flops=mine.size, bytes_accessed=6 * mine.size, transcendentals=0),
        name="round",
    )(place, mine, received)


def prepare_kernel(occ_first, occ_second, vir_col, vir_row, *refs):
    sums, received, base, inverse = refs[:2], refs[2:4], refs[4], refs[5]
    virtual = vir_col.shape[0]
    count = sums[0].shape[0] // virtual
    size = base.shape[0] // count
    for i in range(count):
        rows = slice(i * virtual, (i + 1) * virtual)
        for j in range(2):
            share = 1.0 / (vir_col[...] + vir_row[...] - occ_first[i] - occ_second[j])
            total = (sums[j][rows, :] + received[j][rows, :].astype(F32)) * share
            spread_rows(total, base.at[i * size : (i + 1) * size], j, base.shape[1])
            spread_rows(share, inverse.at[i * size : (i + 1) * size], j, base.shape[1])


def final_kernel(place, base, inverse, early_both, late_same, late_other, out, done, sems):
    size = late_same.shape[0]
    count = done.shape[0] // size
    copies = []
    for orbital in range(count):
        rows = slice(orbital * size, (orbital + 1) * size)
        same = place[0] == orbital // 2
        if orbital % 2 == 0:
            first = pl.ds(pl.multiple_of(jnp.where(same, 0, size), size), size)
            done[rows, :] = base[rows, :] + early_both[first, :].astype(F32) * inverse[rows, :]
        else:

            @pl.when(same)
            def _():
                done[rows, :] = base[rows, :] + late_same[...].astype(F32) * inverse[rows, :]

            @pl.when(jnp.logical_not(same))
            def _():
                done[rows, :] = base[rows, :] + late_other[...].astype(F32) * inverse[rows, :]

        copies.append(pltpu.make_async_copy(done.at[rows, :], out.at[rows, :], sems.at[orbital]))
        copies[-1].start()
    for copy in copies:
        copy.wait()


def inner(amplitudes, factors, occ_energy, vir_energy):
    own_rows, virtual, aux = factors.shape
    pairs_cols = amplitudes.shape[2]
    row, col = lax.axis_index("row"), lax.axis_index("col")
    core, z = lax.rem(col, CORE), col // (X_LO * CORE)
    place = jnp.stack([core, z])
    depth = own_rows * virtual
    half, part = own_rows // 2, virtual // CORE

    piece = lax.dynamic_slice(factors, (z, core * part, 0), (1, part, aux))
    pieces = [send(piece, along_y(s)) for s in (1, -1, 2)]
    left_moved = send(lax.dynamic_slice_in_dim(factors, core * half, half, 0), other_half)

    whole = amplitudes.reshape(depth, pairs_cols * virtual)
    own = [whole[:, j * virtual : (j + 1) * virtual] for j in range(pairs_cols)]
    prev, next_ = [], []
    for j in range(pairs_cols):
        prev.append(send(own[j], along_y(1)))
        next_.append(send(own[j], along_y(-1)))
    pieces = pack(pieces)
    eighths = [pieces] + [send(pieces, along_z(s)) for s in (1, 2, 3)]
    left_swapped = send(left_moved, other_core)
    right_moved = pack(eighths)
    right_swapped = send(right_moved, other_core)
    far = [send(prev[0], along_y(1))]
    far.append(send(next_[1], along_y(-1)))

    count, rest = own_rows, 3 * own_rows
    coupling = {}
    coupling["mine", "own"] = couple(couple_whole_kernel, [factors, factors], count, count, virtual, aux)
    coupling["other", "own"] = couple(
        couple_other_own_kernel, [place, left_moved, left_swapped, factors], count, count, virtual, aux, (count,)
    )
    operands = [place, left_moved, left_swapped, right_moved, right_swapped]
    coupling["other", "rest"] = couple(
        couple_other_rest_kernel, operands, count, rest, virtual, aux, (count, rest)
    )
    operands = [place, factors, right_moved, right_swapped]
    coupling["mine", "rest"] = couple(couple_mine_rest_kernel, operands, count, rest, virtual, aux, (rest,))

    def sums_of(name, j, dtype):
        rest = coupling[name, "rest"]
        pieces = [(rest, 0, prev[j]), (rest, depth, next_[j]), (rest, 2 * depth, far[j])]
        return product([(coupling[name, "own"], 0, own[j]), *pieces], None, dtype)

    sums, received, mirrored = [], [], []
    for j in range(pairs_cols):
        other = sums_of("other", j, BF16)
        received.append(send(other, other_half))
        sums.append(sums_of("mine", j, F32))
    lanes = 128
    cuts = virtual // lanes
    for j in range(pairs_cols):
        same, other = round_halves(place, sums[j], received[j], lanes)
        if j == 0:
            halves = [send(same, spread(0)), send(other, spread(1))]
            mirrored.append(send(pack(halves), mirror_rest))
            continue
        mirrored += [send(same, mirror_whole(0)), send(other, mirror_whole(1))]

    occ_first = lax.dynamic_slice_in_dim(occ_energy, row * own_rows, own_rows, 0)
    occ_second = lax.dynamic_slice_in_dim(occ_energy, col * pairs_cols, pairs_cols, 0)
    shape = jax.ShapeDtypeStruct((depth * cuts * pairs_cols, lanes), F32)
    operands = [vir_energy[:, None], vir_energy[None, :], *sums, *received]
    base, inverse = pl.pallas_call(
        prepare_kernel,
        out_shape=[shape, shape],
        in_specs=[SMEM] * 2 + [VMEM] * len(operands),
        out_specs=[VMEM, VMEM],
        compiler_params=pltpu.CompilerParams(vmem_limit_bytes=4 << 20),
        cost_estimate=pl.CostEstimate(flops=4 * shape.size, bytes_accessed=10 * shape.size, transcendentals=0),
        name="prepare",
    )(occ_first, occ_second, *operands)
    operands = [place, base, inverse, *mirrored]
    specs = [SMEM] + [VMEM] * (len(operands) - 1)
    out = pl.pallas_call(
        final_kernel,
        out_shape=shape,
        in_specs=specs,
        out_specs=pl.BlockSpec(memory_space=pl.ANY),
        scratch_shapes=[pltpu.VMEM(shape.shape, F32), pltpu.SemaphoreType.DMA((own_rows,))],
        compiler_params=pltpu.CompilerParams(vmem_limit_bytes=6 << 20),
        cost_estimate=pl.CostEstimate(flops=2 * shape.size, bytes_accessed=12 * shape.size, transcendentals=0),
        name="finish",
    )(*operands)
    out = out.reshape(own_rows, virtual, cuts, pairs_cols, lanes).transpose(0, 1, 3, 2, 4)
    return out.reshape(own_rows, virtual, pairs_cols, virtual)


def solution(mesh):
    in_specs = (P("row", None, "col", None), P("row", None, None), P(), P())
    out_specs = P("row", None, "col", None)
    return jax.shard_map(inner, mesh=mesh, in_specs=in_specs, out_specs=out_specs, check_vma=False)
```
